32 devices in a mesh: bulk: 4 (over x, core), grid: 8 (over z, y).
Axes of the slice: x: 2, y: 2, z: 4, core: 2. Of those that a mesh axis runs over, the one named last changes fastest.
Arguments:
- offsets: float32 [8, 3, 4, 24, 128], P('grid', None, 'bulk'), may hold values from -0.75 to 0.75
- flow: float32 [8, 5, 4, 24, 128], P('grid', None, 'bulk'), may hold values from -6 to 6
- control_points: float32 [3, 16384], P(None, ('bulk', 'grid')), may hold values from -7 to 13
- rbf_weights: float32 [3, 16384], P(None, ('bulk', 'grid')), may hold values from -2 to 2
- peer_offset: int32 [8, 720, 1], P('grid', 'bulk'), may hold values from 0 to 6; in each aligned block of 180 rows (0 to 179, 180 to 359, ..., all dimensions but the last counted through in order) at most 28 rows name the same one
- donor_block: int32 [8, 720], P('grid', 'bulk'), may hold values from 0 to 23
- receptor_block: int32 [8, 720], P('grid', 'bulk'), may hold values from 0 to 23
Outputs:
- moved: float32 [8, 3, 4, 24, 128], P('grid', None, 'bulk')
- metric: float32 [8, 4, 24, 128], P('grid', 'bulk')
- fringe: float32 [8, 5, 4, 24, 128], P('grid', None, 'bulk')
The draws below stay inside these ranges and needn't reach their ends.
Inputs may be any that keep to these rules, and one draw needn't show every extreme that they name: `peer_offset`: in the 180 rows of one device no value appears more than 28 times.
All inputs are finite; a program needn't handle non-finite values.
Results may differ from the reference program's by a relative error of at most 0.0003.
Values sent between devices are 32-bit elements; how exact they have to be, the bound alone decides.
A program may use at most 64 MiB of HBM per device.

```python
import math
import jax
import jax.numpy as jnp
import numpy as np
from jax import lax

P_SIZE = 16384
VARS = 5
AI = 1
NJ = 24
NK = 128
SLOTS = 180
CAP = 28
G = 8
NI = 4
N_BULK = 4
N_GRID = 8


def draw_control_points(key, part):
    reach = 1.0 + 0.25 * (NJ - 1)
    unit = jax.random.uniform(key, (3, P_SIZE), jnp.float32)
    lower = jnp.array([-reach, -reach, 0.0], jnp.float32)
    upper = jnp.array([0.5 * (G - 1) + reach, reach, 0.1 * (NK - 1)], jnp.float32)
    return lower[:, None] + (upper - lower)[:, None] * unit


def touch_ends(drawn, key, smallest, top_value):
    spot = [jax.random.randint(jax.random.fold_in(key, axis), (), 0, length) for axis, length in enumerate(drawn.shape)]
    longest = drawn.shape.index(max(drawn.shape))
    beside = spot[:longest] + [(spot[longest] + 1) % drawn.shape[longest]] + spot[longest + 1:]
    return drawn.at[tuple(spot)].set(smallest).at[tuple(beside)].set(top_value)


def level_of(rng, extent, shards, least, top_value):
    def one(axis_at, parts):
        steps = jax.random.uniform(jax.random.fold_in(jax.random.fold_in(rng, 6), axis_at), (parts,), jnp.float32, least / len(shards), top_value / len(shards))
        return jnp.repeat(jnp.exp(steps), extent[axis_at] // parts).reshape((-1,) + (1,) * (len(extent) - axis_at - 1))

    loudness = one(*shards[0])
    for cut in shards[1:]:
        loudness = loudness * one(*cut)
    return loudness


def assign_block(stream_key, own, number, rows, amount, top, most, slope):
    ranking = jax.random.permutation(stream_key, amount)
    crowded, common = load_shares(amount, rows * top, most, slope, True), load_shares(amount, rows * top, most, slope, False)
    places = jnp.arange(amount)

    def named(tallies, offset_by):
        used = int((tallies > 0).sum())
        fixed = max(1, used // 4)
        moved = fixed + (places - fixed + offset_by * (used - fixed)) % max(1, amount - fixed)
        return jnp.zeros((amount,), jnp.int32).at[ranking[jnp.where(places < fixed, places, moved)]].set(jnp.asarray(tallies, jnp.int32))

    tallies = jnp.where(number % 4 == 0, named(crowded, number // 4), named(common, number - number // 4 - 1))
    mixed = jax.random.permutation(jax.random.fold_in(own, 3), amount)
    source_of, taker = mixed[0:amount // 2 * 2:2], mixed[1:amount // 2 * 2:2]
    slack = jnp.minimum(tallies[source_of] - 1, most - tallies[taker]) // 2
    slack = jnp.where((source_of == ranking[0]) | (taker == ranking[0]) | (tallies[taker] == 0), 0, jnp.maximum(slack, 0))
    moved = jax.random.randint(jax.random.fold_in(own, 4), (amount // 2,), 0, 1 << 20) % (slack + 1)
    tallies = tallies.at[source_of].add(-moved).at[taker].add(moved)
    members = jnp.searchsorted(jnp.cumsum(tallies), jnp.arange(rows * top), side="right").astype(jnp.int32)
    grid = members.reshape(top, rows).T
    grid = grid[jax.random.permutation(jax.random.fold_in(own, 1), rows)]
    offset_by = jax.random.randint(jax.random.fold_in(own, 2), (rows, 1), 0, top)
    return jnp.take_along_axis(grid, (jnp.arange(top)[None, :] + offset_by) % top, axis=1)


def load_shares(count, total, bound, slope, full):
    loads = [(1 << 20) // math.isqrt(standing ** slope) + 1 for standing in range(1, count + 1)]
    largest = bound if full else min(bound, max(-(-total // count), total * loads[0] // sum(loads)))
    least = 1 if total - largest >= count - 1 else 0
    holding, spare = [largest] + [least] * (count - 1), total - largest - least * (count - 1)
    while spare > 0:
        candidates = [i for i in range(1, count) if holding[i] < largest] or [i for i in range(1, count) if holding[i] < bound]
        whole, remaining = sum([loads[i] for i in candidates]), spare
        for i in candidates:
            addition = min(bound - holding[i], max(1, remaining * loads[i] // whole), spare)
            holding[i] = holding[i] + addition
            spare = spare - addition
    return np.array(holding)


def scatter_about(rng, dims, spread, limit, shards=(), kind=jnp.bfloat16):
    values = jax.random.normal(rng, dims, jnp.float32) * spread
    if len(shards) > 0:
        values = level_of(rng, dims, shards, -0.22, 0.18) * values
    return jnp.clip(values, min=-limit, max=limit).astype(kind)


def setup_inputs(seed: int = 0) -> dict:
    arg_keys = jax.random.split(jax.random.key(seed), 8)
    offsets = scatter_about(arg_keys[0], (G, 3, NI, NJ, NK), 0.05, 0.75, ((0, 8), (2, 4)), jnp.float32)
    flow = scatter_about(arg_keys[1], (G, VARS, NI, NJ, NK), 1.0, 6.0, ((0, 8), (2, 4)), jnp.float32)
    control_points = draw_control_points(jax.random.fold_in(arg_keys[7], 71), 0)
    rbf_weights = scatter_about(arg_keys[3], (3, P_SIZE), 0.15, 2.0, ((1, 32),), jnp.float32)
    peer_offset_keys = jax.random.split(jax.random.fold_in(arg_keys[4], 1), G * (N_BULK * SLOTS) // SLOTS)
    peer_offset_turns = jax.random.permutation(jax.random.fold_in(arg_keys[4], 3), G * (N_BULK * SLOTS) // SLOTS)
    peer_offset = jax.vmap(lambda own, number: assign_block(jax.random.fold_in(arg_keys[4], 2), own, number, SLOTS, N_GRID - 1, 1, CAP, 2))(peer_offset_keys, peer_offset_turns).reshape((G, N_BULK * SLOTS, 1))
    donor_block = touch_ends(jax.random.randint(arg_keys[5], (G, N_BULK * SLOTS), 0, AI * NJ), jax.random.fold_in(arg_keys[5], 1), 0, (AI * NJ) - 1).astype(jnp.int32)
    receptor_block = touch_ends(jax.random.randint(arg_keys[6], (G, N_BULK * SLOTS), 0, AI * NJ), jax.random.fold_in(arg_keys[6], 1), 0, (AI * NJ) - 1).astype(jnp.int32)
    return {"offsets": offsets, "flow": flow, "control_points": control_points, "rbf_weights": rbf_weights, "peer_offset": peer_offset, "donor_block": donor_block, "receptor_block": receptor_block}


HIGHEST = lax.Precision.HIGHEST
SUPPORT = 1.25

def lattice(grid_ids, plane_ids, planes_total, radial, lines):
    theta = 2.0 * math.pi * plane_ids.astype(jnp.float32) / planes_total
    radius = 1.0 + 0.25 * jnp.arange(radial, dtype=jnp.float32)
    height = 0.1 * jnp.arange(lines, dtype=jnp.float32)
    centre = 0.5 * grid_ids.astype(jnp.float32)
    xcoord = centre[:, None, None, None] + radius[None, None, :, None] * jnp.cos(theta)[None, :, None, None] + 0.0 * height[None, None, None, :]
    ycoord = (radius[None, :, None] * jnp.sin(theta)[:, None, None] + 0.0 * height[None, None, :])[None] + 0.0 * centre[:, None, None, None]
    zcoord = jnp.zeros_like(xcoord) + height[None, None, None, :]
    return jnp.stack([xcoord, ycoord, zcoord], axis=1)

def kernel_sum(nodes, points, weights):
    squared = (nodes[0][:, None] - points[0][None, :]) ** 2
    squared = squared + (nodes[1][:, None] - points[1][None, :]) ** 2
    squared = squared + (nodes[2][:, None] - points[2][None, :]) ** 2
    scaled = jnp.sqrt(squared) / SUPPORT
    inside = jnp.maximum(1.0 - scaled, 0.0)
    basis = inside ** 4 * (4.0 * scaled + 1.0)
    return jnp.einsum('ck,nk->cn', weights, basis, precision=HIGHEST)

def along_axis(field, axis):
    total = field.shape[axis]
    ahead = lax.slice_in_dim(field, 2, total, axis=axis)
    behind = lax.slice_in_dim(field, 0, total - 2, axis=axis)
    first = lax.slice_in_dim(field, 1, 2, axis=axis) - lax.slice_in_dim(field, 0, 1, axis=axis)
    last = lax.slice_in_dim(field, total - 1, total, axis=axis) - lax.slice_in_dim(field, total - 2, total - 1, axis=axis)
    return jnp.concatenate([first, (ahead - behind) * 0.5, last], axis=axis)

def jacobian(slope_plane, slope_radial, slope_height):
    cross_x = slope_radial[:, 1] * slope_height[:, 2] - slope_radial[:, 2] * slope_height[:, 1]
    cross_y = slope_radial[:, 2] * slope_height[:, 0] - slope_radial[:, 0] * slope_height[:, 2]
    cross_z = slope_radial[:, 0] * slope_height[:, 1] - slope_radial[:, 1] * slope_height[:, 0]
    return slope_plane[:, 0] * cross_x + slope_plane[:, 1] * cross_y + slope_plane[:, 2] * cross_z

def blend(receptor_xyz, donor_xyz, donor_values):
    squared = (receptor_xyz[:, 0, :, None] - donor_xyz[:, 0, None, :]) ** 2
    squared = squared + (receptor_xyz[:, 1, :, None] - donor_xyz[:, 1, None, :]) ** 2
    squared = squared + (receptor_xyz[:, 2, :, None] - donor_xyz[:, 2, None, :]) ** 2
    weight = 1.0 / (0.25 + squared)
    totals = lax.optimization_barrier(jnp.sum(weight, axis=2))
    weighted = jnp.einsum('nad,nvd->nva', weight, donor_values, precision=HIGHEST)
    return weighted / totals[:, None, :]

def reference(offsets, flow, control_points, rbf_weights, peer_offset, donor_block, receptor_block):
    grids = offsets.shape[0]
    planes = offsets.shape[2]
    base = lattice(jnp.arange(grids, dtype=jnp.int32), jnp.arange(planes, dtype=jnp.int32), planes, NJ, NK) + offsets
    flat = jnp.transpose(base, (1, 0, 2, 3, 4)).reshape(3, -1)
    tile_nodes = NJ * NK
    tiles = jnp.transpose(flat.reshape(3, -1, tile_nodes), (1, 0, 2))
    moves = lax.map(lambda tile: kernel_sum(tile, control_points, rbf_weights), tiles)
    shifts = jnp.transpose(moves, (1, 0, 2)).reshape(3, grids, planes, NJ, NK)
    moved = base + jnp.transpose(shifts, (1, 0, 2, 3, 4))
    wrapped = jnp.concatenate([moved[:, :, -1:], moved, moved[:, :, :1]], axis=2)
    slope_plane = (wrapped[:, :, 2:] - wrapped[:, :, :-2]) * 0.5
    slope_radial = along_axis(moved, 3)
    slope_height = along_axis(moved, 4)
    metric = jacobian(slope_plane, slope_radial, slope_height)
    values = metric[:, None] * flow
    payload = jnp.concatenate([moved, values], axis=1).reshape(grids, 3 + VARS, planes * NJ, NK)
    coords = moved.reshape(grids, 3, planes * NJ, NK)
    entries = peer_offset.shape[1]
    source_grid = jnp.broadcast_to(jnp.arange(grids, dtype=jnp.int32)[:, None], (grids, entries))
    receiver = (source_grid + 1 + peer_offset[:, :, 0]) % grids
    quarter = (jnp.arange(entries, dtype=jnp.int32) // SLOTS)[None, :] * (AI * NJ)
    donor_ids = (quarter + donor_block).reshape(-1, SLOTS)
    receptor_ids = (quarter + receptor_block).reshape(-1, SLOTS)
    source_ids = source_grid.reshape(-1, SLOTS)
    receiver_ids = receiver.reshape(-1, SLOTS)

    def group(items):
        source_now, receiver_now, donor_now, receptor_now = items
        donor = payload[source_now, :, donor_now]
        receptor_xyz = coords[receiver_now, :, receptor_now]
        return blend(receptor_xyz, donor[:, :3], donor[:, 3:])
    pieces = lax.map(group, (source_ids, receiver_ids, donor_ids, receptor_ids))
    pieces = pieces.reshape(-1, VARS, NK)
    fringe = jnp.zeros((grids, VARS, planes * NJ, NK), jnp.float32)
    fringe = fringe.at[receiver_ids.reshape(-1), :, receptor_ids.reshape(-1)].add(pieces)
    return (moved, metric, fringe.reshape(grids, VARS, planes, NJ, NK))
```

```python
import functools
import math

import jax
import jax.numpy as jnp
from jax import lax
from jax.experimental import pallas as pl
from jax.experimental.pallas import tpu as pltpu
from jax.sharding import PartitionSpec as P

MESH = pl.DeviceIdType.MESH
SUPPORT = 1.25
CULL = SUPPORT * SUPPORT * 1.0001
FAR = 1.0e9
UNROLL = 16
ENTRY_UNROLL = 2
F32 = jnp.float32
I32 = jnp.int32
BF16 = jnp.bfloat16
VMEM_SPEC = pl.BlockSpec(memory_space=pltpu.VMEM)
SMEM_SPEC = pl.BlockSpec(memory_space=pltpu.SMEM)


def lattice(grid_ids, plane_ids, planes_total, radial, lines):
    theta = 2.0 * math.pi * plane_ids.astype(jnp.float32) / planes_total
    radius = 1.0 + 0.25 * jnp.arange(radial, dtype=jnp.float32)
    height = 0.1 * jnp.arange(lines, dtype=jnp.float32)
    centre = 0.5 * grid_ids.astype(jnp.float32)
    xcoord = (
        centre[:, None, None, None]
        + radius[None, None, :, None] * jnp.cos(theta)[None, :, None, None]
        + 0.0 * height[None, None, None, :]
    )
    ycoord = (radius[None, :, None] * jnp.sin(theta)[:, None, None] + 0.0 * height[None, None, :])[
        None
    ] + 0.0 * centre[:, None, None, None]
    zcoord = jnp.zeros_like(xcoord) + height[None, None, None, :]
    return jnp.stack([xcoord, ycoord, zcoord], axis=1)


def take_lanes(x, idx):
    dims = lax.GatherDimensionNumbers(
        offset_dims=(),
        collapsed_slice_dims=(1,),
        start_index_map=(1,),
        operand_batching_dims=(0,),
        start_indices_batching_dims=(0,),
    )
    return lax.gather(
        x, idx[..., None], dims, slice_sizes=(1, 1), mode=lax.GatherScatterMode.PROMISE_IN_BOUNDS
    )


def iota(shape, axis):
    return lax.broadcasted_iota(I32, shape, axis)


def search(counts, target):
    pos = jnp.zeros(counts.shape, I32)
    step = counts.shape[1] // 2
    while step:
        seen = take_lanes(counts, pos + (step - 1))
        pos = jnp.where(seen <= target, pos + step, pos)
        step //= 2
    return pos


def gather_kernel(nb, ng, pts_ref, lst_ref, allp_ref, alll_ref, sp, rp, sl, rl):
    b = lax.axis_index("bulk")
    g = lax.axis_index("grid")
    nd = nb * ng
    me = b * ng + g
    barrier = pltpu.get_barrier_semaphore()

    def peer_of(k):
        peer = lax.rem(me + k, nd)
        return (peer // ng, lax.rem(peer, ng))

    @pl.loop(1, nd)
    def _(k):
        pl.semaphore_signal(barrier, inc=1, device_id=peer_of(k), device_id_type=MESH)

    pl.semaphore_wait(barrier, nd - 1)

    def points_copy(k, slot):
        return pltpu.make_async_remote_copy(
            src_ref=pts_ref,
            dst_ref=allp_ref.at[slot],
            send_sem=sp.at[k - 1],
            recv_sem=rp.at[k - 1],
            device_id=peer_of(k),
            device_id_type=MESH,
        )

    def list_copy(k):
        return pltpu.make_async_remote_copy(
            src_ref=lst_ref,
            dst_ref=alll_ref.at[k - 1],
            send_sem=sl.at[k - 1],
            recv_sem=rl.at[k - 1],
            device_id=(b, lax.rem(g + k, ng)),
            device_id_type=MESH,
        )

    @pl.loop(1, nd)
    def _(k):
        points_copy(k, me).start()

    @pl.loop(1, ng)
    def _(k):
        list_copy(k).start()

    allp_ref[me] = pts_ref[...]

    @pl.loop(1, nd)
    def _(k):
        copy = points_copy(k, lax.rem(me + nd - k, nd))
        copy.wait_send()
        copy.wait_recv()

    @pl.loop(1, ng)
    def _(k):
        copy = list_copy(k)
        copy.wait_send()
        copy.wait_recv()


def rbf_kernel(
    nd,
    rows,
    ng,
    lrows,
    base_ref,
    pts_ref,
    lst_ref,
    moved_ref,
    don_ref,
    rec_ref,
    num_ref,
    pnt,
    fil,
    node,
    box,
    out,
    basec,
    cntv,
    cnts,
    shift,
    names,
    sem,
):
    radial = base_ref.shape[1]
    npat = radial
    lane8 = iota((8, 128), 1)
    sub8 = iota((8, 128), 0)
    blocks_of_lanes = lane8 // 16
    within = lane8 - 16 * blocks_of_lanes
    upper = (iota((128, 128), 0) <= iota((128, 128), 1)).astype(F32).astype(BF16)

    def running(mask):
        return jnp.dot(
            mask.astype(F32).astype(BF16), upper, preferred_element_type=F32
        ).astype(I32)

    nrow = (ng - 1) * lrows
    for k in range(ng - 1):
        for c in range(3):
            names[c, k * lrows : (k + 1) * lrows, :] = lst_ref[k, c * lrows : (c + 1) * lrows, :]
    owner = iota((nrow, 128), 0) // lrows
    counts = running(names[0] == owner)
    pos = search(counts, iota((nrow, 128), 1))
    don_ref[...] = owner * radial + take_lanes(names[1], pos)
    rec_ref[...] = take_lanes(names[2], pos)
    num_ref[...] = take_lanes(counts, jnp.full((nrow, 128), 127, I32))

    for d in range(nd):
        for c in range(6):
            pnt[c, d * rows : (d + 1) * rows, :] = pts_ref[d, c * rows : (c + 1) * rows, :]

    lows, highs = [], []
    for c in range(3):
        for jg in range(radial // 8):
            v = base_ref[c, 8 * jg : 8 * jg + 8, :]
            got = jnp.zeros((8, 128), F32)
            for j in range(8):
                row = jnp.broadcast_to(v[j : j + 1, :], (8, 128))
                got = jnp.where(blocks_of_lanes == j, take_lanes(row, 16 * sub8 + within), got)
            node[c, 8 * jg : 8 * jg + 8, :] = got
        full = node[c]
        lo = jnp.min(full, axis=1, keepdims=True)
        hi = jnp.max(full, axis=1, keepdims=True)
        box[2 * c] = jnp.broadcast_to(lo[:, :, None], (npat, 8, 128))
        box[2 * c + 1] = jnp.broadcast_to(hi[:, :, None], (npat, 8, 128))
        lows.append(jnp.min(lo, axis=0, keepdims=True))
        highs.append(jnp.max(hi, axis=0, keepdims=True))

    dist = jnp.zeros((128, 128), F32)
    for c in range(3):
        p = pnt[c]
        e = jnp.maximum(jnp.maximum(lows[c] - p, p - highs[c]), 0.0)
        dist = dist + e * e
    counts = running(dist < CULL)
    lane = iota((128, 128), 1)
    pos = search(counts, lane)
    total = take_lanes(counts, jnp.full((128, 128), 127, I32))
    for c in range(6):
        v = take_lanes(pnt[c], pos)
        v = jnp.where(lane < total, v, FAR if c < 3 else 0.0)
        fil[c] = v.T
    groups = (jnp.max(total) + 7) // 8

    shift[...] = jnp.zeros(shift.shape, F32)
    wide = npat * 8
    lane_w = iota((wide, 128), 1)

    def page_body(state):
        page, _ = state
        basec[...] = jnp.zeros(basec.shape, I32)
        out[...] = jnp.zeros(out.shape, F32)

        @pl.loop(0, groups)
        def _(gi):
            start = pl.multiple_of(gi * 8, 8)
            dist = jnp.zeros((npat, 8, 128), F32)
            for c in range(3):
                p = fil[c, pl.ds(start, 8), :][None]
                e = jnp.maximum(jnp.maximum(box[2 * c] - p, p - box[2 * c + 1]), 0.0)
                dist = dist + e * e
            before = basec[...]
            counts = before + running((dist < CULL).astype(F32).reshape(wide, 128))
            target = lane_w + 128 * page
            pos = search(counts, target)
            after = take_lanes(counts, jnp.full((wide, 128), 127, I32))
            keep = jnp.logical_and(target >= before, target < after)
            for c in range(6):
                src = jnp.broadcast_to(
                    fil[c, pl.ds(start, 8), :][None], (npat, 8, 128)
                ).reshape(wide, 128)
                out[c] = jnp.where(keep, take_lanes(src, pos), out[c])
            basec[...] = after

        most = jnp.max(basec[...].reshape(npat, 8, 128), axis=1)
        cntv[...] = most
        copy = pltpu.make_async_copy(cntv, cnts, sem)
        copy.start()
        copy.wait()

        @pl.loop(0, npat)
        def _(p):
            n = jnp.minimum(cnts[p, 0] - 128 * page, 128)
            turns = (jnp.maximum(n, 0) + (UNROLL - 1)) // UNROLL
            at = [jnp.broadcast_to(node[c, pl.ds(p, 1), :] * 0.8, (8, 128)) for c in range(3)]
            first = pl.multiple_of(p * 8, 8)
            cols = [out[c, pl.ds(first, 8), :] for c in range(6)]
            cols = [v * 0.8 for v in cols[:3]] + cols[3:]

            def step(i, acc):
                acc = list(acc)
                for u in range(UNROLL):
                    idx = jnp.full((8, 128), i * UNROLL + u, I32)
                    px, py, pz, wx, wy, wz = [take_lanes(v, idx) for v in cols]
                    dx = at[0] - px
                    dy = at[1] - py
                    dz = at[2] - pz
                    sq = jnp.maximum(dx * dx + dy * dy + dz * dz, 1e-30)
                    near = jnp.maximum(1.0 - sq * lax.rsqrt(sq), 0.0)
                    two = near * near
                    phi = two * two * (5.0 - 4.0 * near)
                    acc = [acc[0] + wx * phi, acc[1] + wy * phi, acc[2] + wz * phi]
                return tuple(acc)

            zero = jnp.zeros((8, 128), F32)
            acc = lax.fori_loop(0, turns, step, (zero, zero, zero))
            for c in range(3):
                shift[c, pl.ds(p, 1), :] += jnp.sum(acc[c], axis=0, keepdims=True)

        return page + 1, jnp.max(most)

    lax.while_loop(
        lambda state: state[0] * 128 < state[1], page_body, (jnp.int32(0), jnp.int32(1))
    )

    for c in range(3):
        for jg in range(radial // 8):
            s = shift[c, 8 * jg : 8 * jg + 8, :]
            got = jnp.zeros((8, 128), F32)
            for kg in range(8):
                row = jnp.broadcast_to(s[kg : kg + 1, :], (8, 128))
                got = jnp.where(blocks_of_lanes == kg, take_lanes(row, 16 * sub8 + within), got)
            moved_ref[c, 8 * jg : 8 * jg + 8, :] = base_ref[c, 8 * jg : 8 * jg + 8, :] + got


def metric_kernel(nb, ng, mov_ref, met_ref, allm_ref, allt_ref, halo, sh, rh, sm, rm, st, rt):
    b = lax.axis_index("bulk")
    g = lax.axis_index("grid")
    after = lax.rem(b + 1, nb)
    before = lax.rem(b + nb - 1, nb)
    barrier = pltpu.get_barrier_semaphore()
    for t in (before, after):
        pl.semaphore_signal(barrier, inc=1, device_id=(t, g), device_id_type=MESH)
    for k in range(1, ng):
        pl.semaphore_signal(
            barrier, inc=1, device_id=(b, lax.rem(g + k, ng)), device_id_type=MESH
        )
    pl.semaphore_wait(barrier, 2 + ng - 1)
    halos = [
        pltpu.make_async_remote_copy(
            src_ref=mov_ref,
            dst_ref=halo.at[i],
            send_sem=sh.at[i],
            recv_sem=rh.at[i],
            device_id=(t, g),
            device_id_type=MESH,
        )
        for i, t in enumerate((after, before))
    ]
    for copy in halos:
        copy.start()

    def to_peers(src, dst, ss, rs):
        return [
            pltpu.make_async_remote_copy(
                src_ref=src,
                dst_ref=dst.at[k - 1],
                send_sem=ss.at[k - 1],
                recv_sem=rs.at[k - 1],
                device_id=(b, lax.rem(g + k, ng)),
                device_id_type=MESH,
            )
            for k in range(1, ng)
        ]

    nodes = to_peers(mov_ref, allm_ref, sm, rm)
    for copy in nodes:
        copy.start()
    radial, lines = mov_ref.shape[1:]
    row = iota((radial, lines), 0)
    col = iota((radial, lines), 1)
    dj, dk = [], []
    for c in range(3):
        m = mov_ref[c]
        up, down = pltpu.roll(m, radial - 1, 0), pltpu.roll(m, 1, 0)
        dj.append(
            jnp.where(row == 0, up - m, jnp.where(row == radial - 1, m - down, (up - down) * 0.5))
        )
        up, down = pltpu.roll(m, lines - 1, 1), pltpu.roll(m, 1, 1)
        dk.append(
            jnp.where(col == 0, up - m, jnp.where(col == lines - 1, m - down, (up - down) * 0.5))
        )
    cross = [
        dj[1] * dk[2] - dj[2] * dk[1],
        dj[2] * dk[0] - dj[0] * dk[2],
        dj[0] * dk[1] - dj[1] * dk[0],
    ]
    for copy in halos:
        copy.wait_recv()
    di = [(halo[1, c] - halo[0, c]) * 0.5 for c in range(3)]
    met_ref[...] = di[0] * cross[0] + di[1] * cross[1] + di[2] * cross[2]
    mets = to_peers(met_ref, allt_ref, st, rt)
    for copy in mets:
        copy.start()
    for copy in halos:
        copy.wait_send()
    for copy in nodes + mets:
        copy.wait_send()
        copy.wait_recv()


def blend_kernel(
    don_ref, rec_ref, num_ref, mov_ref, allm_ref, allt_ref, flow_ref, out_ref, rep, tr, acc
):
    radial = mov_ref.shape[1]
    nvar = out_ref.shape[0]
    nrow = num_ref.shape[0]
    sub8 = iota((8, 128), 0)
    for c in range(3):
        tr[c] = jnp.zeros((128, 128), F32)
        tr[c, 0:radial, :] = mov_ref[c]
        tr[c] = tr[c].T

    @pl.loop(0, radial)
    def _(blk):
        idx = jnp.full((128, 128), blk, I32)
        for c in range(3):
            rep[blk, c] = take_lanes(tr[c], idx)

    acc[...] = jnp.zeros(acc.shape, F32)

    @pl.loop(0, nrow)
    def _(r):
        n = num_ref[r, 0]

        @pl.loop(0, (n + ENTRY_UNROLL - 1) // ENTRY_UNROLL)
        def _(i):
            found = []
            for u in range(ENTRY_UNROLL):
                e = i * ENTRY_UNROLL + u
                code = don_ref[r, e]
                recv = rec_ref[r, e]
                k = code // radial
                d = code - k * radial
                sq = None
                for c in range(3):
                    diff = rep[recv, c] - allm_ref[k, c, pl.ds(d, 1), :]
                    sq = diff * diff if sq is None else sq + diff * diff
                w = 1.0 / (0.25 + sq)
                hi = w.astype(BF16)
                lo = (w - hi.astype(F32)).astype(BF16)
                vals = jnp.where(sub8 == nvar, 1.0, jnp.zeros((8, 128), F32))
                met = allt_ref[k, pl.ds(d, 1), :]
                for v in range(nvar):
                    row = met * flow_ref[k, v, pl.ds(d, 1), :]
                    vals = jnp.where(sub8 == v, row, vals)
                vhi = vals.astype(BF16).astype(F32)
                both = jnp.concatenate([vhi, vals - vhi], axis=0).astype(BF16)
                got = lax.dot_general(
                    jnp.concatenate([both, both], axis=1),
                    jnp.concatenate([hi, lo], axis=1),
                    (((1,), (1,)), ((), ())),
                    preferred_element_type=F32,
                )
                got = got[0:8] + got[8:16]
                got = got / got[nvar : nvar + 1, :]
                found.append((recv, jnp.where(e < n, got, 0.0)))
            for recv, got in found:
                first = pl.multiple_of(recv * 8, 8)
                acc[pl.ds(first, 8), :] += got

    for v in range(nvar):
        out_ref[v] = acc[pl.ds(v, radial, stride=8), :]


def local(offsets, flow, control_points, rbf_weights, peer_offset, donor_block, receptor_block):
    _, _, planes, radial, lines = offsets.shape
    nvar = flow.shape[1]
    nb = lax.axis_size("bulk")
    ng = lax.axis_size("grid")
    nd = nb * ng
    grid_here = lax.axis_index("grid")
    plane_ids = lax.axis_index("bulk") * planes + jnp.arange(planes, dtype=I32)
    base = lattice(grid_here[None], plane_ids, planes * nb, radial, lines) + offsets
    base = base.reshape(3, radial, lines)
    rows = control_points.shape[1] // 128
    points = jnp.concatenate([control_points, rbf_weights], axis=0).reshape(6 * rows, 128)
    slots = donor_block.shape[1]
    lrows = -(-slots // 128)
    spare = lrows * 128 - slots

    def lanes(x, fill):
        return jnp.pad(x.reshape(-1), (0, spare), constant_values=fill).reshape(lrows, 128)

    lists = jnp.concatenate(
        [lanes(peer_offset, -1), lanes(donor_block, 0), lanes(receptor_block, 0)], axis=0
    )
    dma = pltpu.SemaphoreType.DMA
    sds = jax.ShapeDtypeStruct
    allp, alll = pl.pallas_call(
        functools.partial(gather_kernel, nb, ng),
        out_shape=(sds((nd, 6 * rows, 128), F32), sds((ng - 1, 3 * lrows, 128), I32)),
        in_specs=[VMEM_SPEC] * 2,
        out_specs=[VMEM_SPEC] * 2,
        scratch_shapes=[dma((nd - 1,)), dma((nd - 1,)), dma((ng - 1,)), dma((ng - 1,))],
        compiler_params=pltpu.CompilerParams(collective_id=0, has_side_effects=True),
        name="gather_points",
    )(points, lists)
    plain = flow.reshape(nvar, radial, lines)
    flows = jnp.stack(
        [
            lax.ppermute(plain, "grid", [(i, (i + k) % ng) for i in range(ng)])
            for k in range(1, ng)
        ]
    )
    nrow = (ng - 1) * lrows
    moved, don, rec, num = pl.pallas_call(
        functools.partial(rbf_kernel, nd, rows, ng, lrows),
        out_shape=(
            sds((3, radial, lines), F32),
            sds((nrow, 128), I32),
            sds((nrow, 128), I32),
            sds((nrow, 128), I32),
        ),
        in_specs=[VMEM_SPEC] * 3,
        out_specs=[VMEM_SPEC] * 4,
        scratch_shapes=[
            pltpu.VMEM((6, nd * rows, 128), F32),
            pltpu.VMEM((6, 128, 128), F32),
            pltpu.VMEM((3, radial, 128), F32),
            pltpu.VMEM((6, radial, 8, 128), F32),
            pltpu.VMEM((6, radial * 8, 128), F32),
            pltpu.VMEM((radial * 8, 128), I32),
            pltpu.VMEM((radial, 128), I32),
            pltpu.SMEM((radial, 128), I32),
            pltpu.VMEM((3, radial, 128), F32),
            pltpu.VMEM((3, nrow, 128), I32),
            dma,
        ],
        cost_estimate=pl.CostEstimate(flops=200000000, bytes_accessed=500000, transcendentals=0),
        name="move_nodes",
    )(base, allp, alll)
    metric, allm, allt = pl.pallas_call(
        functools.partial(metric_kernel, nb, ng),
        out_shape=(
            sds((radial, lines), F32),
            sds((ng - 1, 3, radial, lines), F32),
            sds((ng - 1, radial, lines), F32),
        ),
        in_specs=[VMEM_SPEC],
        out_specs=[VMEM_SPEC] * 3,
        scratch_shapes=[
            pltpu.VMEM((2, 3, radial, lines), F32),
            dma((2,)),
            dma((2,)),
            dma((ng - 1,)),
            dma((ng - 1,)),
            dma((ng - 1,)),
            dma((ng - 1,)),
        ],
        compiler_params=pltpu.CompilerParams(collective_id=1, has_side_effects=True),
        name="metric",
    )(moved)
    fringe = pl.pallas_call(
        blend_kernel,
        out_shape=sds((nvar, radial, lines), F32),
        in_specs=[SMEM_SPEC] * 3 + [VMEM_SPEC] * 4,
        out_specs=VMEM_SPEC,
        scratch_shapes=[
            pltpu.VMEM((radial, 3, 128, 128), F32),
            pltpu.VMEM((3, 128, 128), F32),
            pltpu.VMEM((radial * 8, 128), F32),
        ],
        name="blend",
    )(don, rec, num, moved, allm, allt, flows)
    return (
        moved.reshape(1, 3, planes, radial, lines),
        metric.reshape(1, planes, radial, lines),
        fringe.reshape(1, nvar, planes, radial, lines),
    )


def solution(mesh):
    in_specs = (
        P("grid", None, "bulk", None, None),
        P("grid", None, "bulk", None, None),
        P(None, ("bulk", "grid")),
        P(None, ("bulk", "grid")),
        P("grid", "bulk", None),
        P("grid", "bulk"),
        P("grid", "bulk"),
    )
    out_specs = (
        P("grid", None, "bulk", None, None),
        P("grid", "bulk", None, None),
        P("grid", None, "bulk", None, None),
    )
    return jax.shard_map(local, mesh=mesh, in_specs=in_specs, out_specs=out_specs, check_vma=False)
```

```python
import functools
import math

import jax
import jax.numpy as jnp
from jax import lax
from jax.experimental import pallas as pl
from jax.experimental.pallas import tpu as pltpu
from jax.sharding import PartitionSpec as P

MESH = pl.DeviceIdType.MESH
SUPPORT = 1.25
CULL = SUPPORT * SUPPORT * 1.0001
FAR = 1.0e9
UNROLL = 16
ENTRY_UNROLL = 4
F32 = jnp.float32
I32 = jnp.int32
BF16 = jnp.bfloat16
VMEM_SPEC = pl.BlockSpec(memory_space=pltpu.VMEM)
SMEM_SPEC = pl.BlockSpec(memory_space=pltpu.SMEM)


def lattice(grid_ids, plane_ids, planes_total, radial, lines):
    theta = 2.0 * math.pi * plane_ids.astype(jnp.float32) / planes_total
    radius = 1.0 + 0.25 * jnp.arange(radial, dtype=jnp.float32)
    height = 0.1 * jnp.arange(lines, dtype=jnp.float32)
    centre = 0.5 * grid_ids.astype(jnp.float32)
    xcoord = (
        centre[:, None, None, None]
        + radius[None, None, :, None] * jnp.cos(theta)[None, :, None, None]
        + 0.0 * height[None, None, None, :]
    )
    ycoord = (radius[None, :, None] * jnp.sin(theta)[:, None, None] + 0.0 * height[None, None, :])[
        None
    ] + 0.0 * centre[:, None, None, None]
    zcoord = jnp.zeros_like(xcoord) + height[None, None, None, :]
    return jnp.stack([xcoord, ycoord, zcoord], axis=1)


def take_lanes(x, idx):
    dims = lax.GatherDimensionNumbers(
        offset_dims=(),
        collapsed_slice_dims=(1,),
        start_index_map=(1,),
        operand_batching_dims=(0,),
        start_indices_batching_dims=(0,),
    )
    return lax.gather(
        x, idx[..., None], dims, slice_sizes=(1, 1), mode=lax.GatherScatterMode.PROMISE_IN_BOUNDS
    )


def iota(shape, axis):
    return lax.broadcasted_iota(I32, shape, axis)


def search(counts, target):
    pos = jnp.zeros(counts.shape, I32)
    step = counts.shape[1] // 2
    while step:
        seen = take_lanes(counts, pos + (step - 1))
        pos = jnp.where(seen <= target, pos + step, pos)
        step //= 2
    return pos


def halves(n):
    return (n // 2, 2) if n % 2 == 0 else (n, 1)


def line_and_pair(me, n):
    high, low = halves(n)
    place = lax.rem(me, low)
    line = [lax.rem(me // low + m, high) * low + place for m in range(1, high)]
    pair = [me + 1 - 2 * place] if low == 2 else []
    return line, pair


def gather_kernel(
    nb, ng, pts_ref, lst_ref, flow_ref, allp_ref, alll_ref, allf_ref, sp, rp, sl, rl, sf, rf
):
    b = lax.axis_index("bulk")
    g = lax.axis_index("grid")
    gline, gpair = line_and_pair(g, ng)
    bline, bpair = line_and_pair(b, nb)
    barrier = pltpu.get_barrier_semaphore()
    peers = [(b, t) for t in gline + gpair] + [(t, g) for t in bline + bpair]
    for peer in peers:
        pl.semaphore_signal(barrier, inc=1, device_id=peer, device_id_type=MESH)
    pl.semaphore_wait(barrier, len(peers))
    sent = {"p": [], "l": [], "f": []}

    def send(kind, slot, peer, own):
        source, full, ss, rs = {
            "p": (pts_ref, allp_ref, sp, rp),
            "l": (lst_ref, alll_ref, sl, rl),
            "f": (flow_ref, allf_ref, sf, rf),
        }[kind]
        copy = pltpu.make_async_remote_copy(
            src_ref=source if own else full.at[slot],
            dst_ref=full.at[slot],
            send_sem=ss.at[len(sent[kind])],
            recv_sem=rs.at[slot],
            device_id=peer,
            device_id_type=MESH,
        )
        copy.start()
        sent[kind].append(copy)

    def arrived(kind, slot):
        full, ss, rs = {
            "p": (allp_ref, sp, rp),
            "l": (alll_ref, sl, rl),
            "f": (allf_ref, sf, rf),
        }[kind]
        pltpu.make_async_remote_copy(
            src_ref=full.at[slot],
            dst_ref=full.at[slot],
            send_sem=ss.at[0],
            recv_sem=rs.at[slot],
            device_id=peers[0],
            device_id_type=MESH,
        ).wait_recv()

    def across(s, own):
        for t in bline + bpair:
            send("p", b * ng + s, (t, g), own)

    for t in gline + gpair:
        send("p", b * ng + g, (b, t), True)
    across(g, True)
    for kind in ("l", "f"):
        for t in gline + gpair:
            send(kind, g, (b, t), True)
    allp_ref[b * ng + g] = pts_ref[...]
    alll_ref[g] = lst_ref[...]
    for s in gline:
        arrived("p", b * ng + s)
        for t in gpair:
            send("p", b * ng + s, (b, t), False)
        across(s, False)
    for s in gline:
        for kind in ("l", "f"):
            arrived(kind, s)
            for t in gpair:
                send(kind, s, (b, t), False)
    low = halves(ng)[1]
    other = gpair + [t + gpair[0] - g for t in gline] if low == 2 else []
    for s in other:
        arrived("p", b * ng + s)
        across(s, False)
    for x in bline:
        for s in [g] + gline + other:
            arrived("p", x * ng + s)
            for t in bpair:
                send("p", x * ng + s, (t, g), False)
    for t in bpair:
        for x in [t] + [u + t - b for u in bline]:
            for s in [g] + gline + other:
                arrived("p", x * ng + s)
    for s in other:
        arrived("l", s)
        arrived("f", s)
    for kind in sent:
        for copy in sent[kind]:
            copy.wait_send()


def rbf_kernel(
    nd,
    rows,
    ng,
    lrows,
    here_ref,
    base_ref,
    pts_ref,
    lst_ref,
    moved_ref,
    don_ref,
    rec_ref,
    num_ref,
    pnt,
    fil,
    node,
    box,
    out,
    basec,
    cntv,
    cnts,
    shift,
    names,
    sem,
):
    radial = base_ref.shape[1]
    npat = radial
    lane8 = iota((8, 128), 1)
    sub8 = iota((8, 128), 0)
    blocks_of_lanes = lane8 // 16
    within = lane8 - 16 * blocks_of_lanes
    upper = (iota((128, 128), 0) <= iota((128, 128), 1)).astype(F32).astype(BF16)

    def running(mask):
        return jnp.dot(
            mask.astype(F32).astype(BF16), upper, preferred_element_type=F32
        ).astype(I32)

    nrow = ng * lrows
    for k in range(ng):
        for c in range(3):
            names[c, k * lrows : (k + 1) * lrows, :] = lst_ref[k, c * lrows : (c + 1) * lrows, :]
    owner = iota((nrow, 128), 0) // lrows
    target = owner + 1 + names[0]
    target = jnp.where(target >= ng, target - ng, target)
    counts = running(target == here_ref[0])
    pos = search(counts, iota((nrow, 128), 1))
    don_ref[...] = owner * radial + take_lanes(names[1], pos)
    rec_ref[...] = take_lanes(names[2], pos)
    num_ref[...] = take_lanes(counts, jnp.full((nrow, 128), 127, I32))

    for d in range(nd):
        for c in range(6):
            pnt[c, d * rows : (d + 1) * rows, :] = pts_ref[d, c * rows : (c + 1) * rows, :]

    lows, highs = [], []
    for c in range(3):
        for jg in range(radial // 8):
            v = base_ref[c, 8 * jg : 8 * jg + 8, :]
            got = jnp.zeros((8, 128), F32)
            for j in range(8):
                row = jnp.broadcast_to(v[j : j + 1, :], (8, 128))
                got = jnp.where(blocks_of_lanes == j, take_lanes(row, 16 * sub8 + within), got)
            node[c, 8 * jg : 8 * jg + 8, :] = got
        full = node[c]
        lo = jnp.min(full, axis=1, keepdims=True)
        hi = jnp.max(full, axis=1, keepdims=True)
        box[2 * c] = jnp.broadcast_to(lo[:, :, None], (npat, 8, 128))
        box[2 * c + 1] = jnp.broadcast_to(hi[:, :, None], (npat, 8, 128))
        lows.append(jnp.min(lo, axis=0, keepdims=True))
        highs.append(jnp.max(hi, axis=0, keepdims=True))

    dist = jnp.zeros((128, 128), F32)
    for c in range(3):
        p = pnt[c]
        e = jnp.maximum(jnp.maximum(lows[c] - p, p - highs[c]), 0.0)
        dist = dist + e * e
    counts = running(dist < CULL)
    lane = iota((128, 128), 1)
    pos = search(counts, lane)
    total = take_lanes(counts, jnp.full((128, 128), 127, I32))
    for c in range(6):
        v = take_lanes(pnt[c], pos)
        v = jnp.where(lane < total, v, FAR if c < 3 else 0.0)
        fil[c] = v.T
    groups = (jnp.max(total) + 7) // 8

    shift[...] = jnp.zeros(shift.shape, F32)
    wide = npat * 8
    lane_w = iota((wide, 128), 1)

    def page_body(state):
        page, _ = state
        basec[...] = jnp.zeros(basec.shape, I32)
        out[...] = jnp.zeros(out.shape, F32)

        @pl.loop(0, groups)
        def _(gi):
            start = pl.multiple_of(gi * 8, 8)
            dist = jnp.zeros((npat, 8, 128), F32)
            for c in range(3):
                p = fil[c, pl.ds(start, 8), :][None]
                e = jnp.maximum(jnp.maximum(box[2 * c] - p, p - box[2 * c + 1]), 0.0)
                dist = dist + e * e
            before = basec[...]
            counts = before + running((dist < CULL).astype(F32).reshape(wide, 128))
            target = lane_w + 128 * page
            pos = search(counts, target)
            after = take_lanes(counts, jnp.full((wide, 128), 127, I32))
            keep = jnp.logical_and(target >= before, target < after)
            for c in range(6):
                src = jnp.broadcast_to(
                    fil[c, pl.ds(start, 8), :][None], (npat, 8, 128)
                ).reshape(wide, 128)
                out[c] = jnp.where(keep, take_lanes(src, pos), out[c])
            basec[...] = after

        most = jnp.max(basec[...].reshape(npat, 8, 128), axis=1)
        cntv[...] = most
        copy = pltpu.make_async_copy(cntv, cnts, sem)
        copy.start()
        copy.wait()

        @pl.loop(0, npat)
        def _(p):
            n = jnp.minimum(cnts[p, 0] - 128 * page, 128)
            turns = (jnp.maximum(n, 0) + (UNROLL - 1)) // UNROLL
            at = [jnp.broadcast_to(node[c, pl.ds(p, 1), :] * 0.8, (8, 128)) for c in range(3)]
            first = pl.multiple_of(p * 8, 8)
            cols = [out[c, pl.ds(first, 8), :] for c in range(6)]
            cols = [v * 0.8 for v in cols[:3]] + cols[3:]

            def step(i, acc):
                acc = list(acc)
                for u in range(UNROLL):
                    idx = jnp.full((8, 128), i * UNROLL + u, I32)
                    px, py, pz, wx, wy, wz = [take_lanes(v, idx) for v in cols]
                    dx = at[0] - px
                    dy = at[1] - py
                    dz = at[2] - pz
                    sq = jnp.maximum(dx * dx + dy * dy + dz * dz, 1e-30)
                    near = jnp.maximum(1.0 - sq * lax.rsqrt(sq), 0.0)
                    two = near * near
                    phi = two * two * (5.0 - 4.0 * near)
                    acc = [acc[0] + wx * phi, acc[1] + wy * phi, acc[2] + wz * phi]
                return tuple(acc)

            zero = jnp.zeros((8, 128), F32)
            acc = lax.fori_loop(0, turns, step, (zero, zero, zero))
            for c in range(3):
                shift[c, pl.ds(p, 1), :] += jnp.sum(acc[c], axis=0, keepdims=True)

        return page + 1, jnp.max(most)

    lax.while_loop(
        lambda state: state[0] * 128 < state[1], page_body, (jnp.int32(0), jnp.int32(1))
    )

    for c in range(3):
        for jg in range(radial // 8):
            s = shift[c, 8 * jg : 8 * jg + 8, :]
            got = jnp.zeros((8, 128), F32)
            for kg in range(8):
                row = jnp.broadcast_to(s[kg : kg + 1, :], (8, 128))
                got = jnp.where(blocks_of_lanes == kg, take_lanes(row, 16 * sub8 + within), got)
            moved_ref[c, 8 * jg : 8 * jg + 8, :] = base_ref[c, 8 * jg : 8 * jg + 8, :] + got


def metric_kernel(nb, ng, mov_ref, met_ref, allm_ref, allt_ref, halo, sh, rh, sm, rm, st, rt):
    b = lax.axis_index("bulk")
    g = lax.axis_index("grid")
    after = lax.rem(b + 1, nb)
    before = lax.rem(b + nb - 1, nb)
    barrier = pltpu.get_barrier_semaphore()
    gline, gpair = line_and_pair(g, ng)
    peers = [(before, g), (after, g)] + [(b, t) for t in gline + gpair]
    for peer in peers:
        pl.semaphore_signal(barrier, inc=1, device_id=peer, device_id_type=MESH)
    pl.semaphore_wait(barrier, len(peers))
    halos = [
        pltpu.make_async_remote_copy(
            src_ref=mov_ref,
            dst_ref=halo.at[i],
            send_sem=sh.at[i],
            recv_sem=rh.at[i],
            device_id=(t, g),
            device_id_type=MESH,
        )
        for i, t in enumerate((after, before))
    ]
    for copy in halos:
        copy.start()

    sent = {"m": [], "t": []}

    def describe(kind, slot, peer, own, n):
        source, full, ss, rs = {
            "m": (mov_ref, allm_ref, sm, rm),
            "t": (met_ref, allt_ref, st, rt),
        }[kind]
        return pltpu.make_async_remote_copy(
            src_ref=source if own else full.at[slot],
            dst_ref=full.at[slot],
            send_sem=ss.at[n],
            recv_sem=rs.at[slot],
            device_id=peer,
            device_id_type=MESH,
        )

    def send(kind, slot, peer, own):
        copy = describe(kind, slot, peer, own, len(sent[kind]))
        copy.start()
        sent[kind].append(copy)

    for t in gline + gpair:
        send("m", g, (b, t), True)
    radial, lines = mov_ref.shape[1:]
    row = iota((radial, lines), 0)
    col = iota((radial, lines), 1)
    dj, dk = [], []
    for c in range(3):
        m = mov_ref[c]
        up, down = pltpu.roll(m, radial - 1, 0), pltpu.roll(m, 1, 0)
        dj.append(
            jnp.where(row == 0, up - m, jnp.where(row == radial - 1, m - down, (up - down) * 0.5))
        )
        up, down = pltpu.roll(m, lines - 1, 1), pltpu.roll(m, 1, 1)
        dk.append(
            jnp.where(col == 0, up - m, jnp.where(col == lines - 1, m - down, (up - down) * 0.5))
        )
    cross = [
        dj[1] * dk[2] - dj[2] * dk[1],
        dj[2] * dk[0] - dj[0] * dk[2],
        dj[0] * dk[1] - dj[1] * dk[0],
    ]
    for copy in halos:
        copy.wait_recv()
    di = [(halo[1, c] - halo[0, c]) * 0.5 for c in range(3)]
    met_ref[...] = di[0] * cross[0] + di[1] * cross[1] + di[2] * cross[2]
    for t in gline + gpair:
        send("t", g, (b, t), True)
    for kind in ("m", "t"):
        for s in gline:
            describe(kind, s, peers[0], False, 0).wait_recv()
            for t in gpair:
                send(kind, s, (b, t), False)
    other = gpair + [t + gpair[0] - g for t in gline] if gpair else []
    for kind in ("m", "t"):
        for s in other:
            describe(kind, s, peers[0], False, 0).wait_recv()
    for copy in halos + sent["m"] + sent["t"]:
        copy.wait_send()


def blend_kernel(
    don_ref, rec_ref, num_ref, mov_ref, allm_ref, allt_ref, flow_ref, out_ref, rep, tr, acc
):
    radial = mov_ref.shape[1]
    nvar = out_ref.shape[0]
    nrow = num_ref.shape[0]
    sub8 = iota((8, 128), 0)
    for c in range(3):
        tr[c] = jnp.zeros((128, 128), F32)
        tr[c, 0:radial, :] = mov_ref[c]
        tr[c] = tr[c].T

    @pl.loop(0, radial)
    def _(blk):
        idx = jnp.full((128, 128), blk, I32)
        for c in range(3):
            rep[blk, c] = take_lanes(tr[c], idx)

    acc[...] = jnp.zeros(acc.shape, F32)

    @pl.loop(0, nrow)
    def _(r):
        n = num_ref[r, 0]

        @pl.loop(0, (n + ENTRY_UNROLL - 1) // ENTRY_UNROLL)
        def _(i):
            found = []
            for u in range(ENTRY_UNROLL):
                e = i * ENTRY_UNROLL + u
                code = don_ref[r, e]
                recv = rec_ref[r, e]
                k = code // radial
                d = code - k * radial
                sq = None
                for c in range(3):
                    diff = rep[recv, c] - allm_ref[k, c, pl.ds(d, 1), :]
                    sq = diff * diff if sq is None else sq + diff * diff
                w = 1.0 / (0.25 + sq)
                hi = w.astype(BF16)
                lo = (w - hi.astype(F32)).astype(BF16)
                vals = jnp.where(sub8 == nvar, 1.0, jnp.zeros((8, 128), F32))
                met = allt_ref[k, pl.ds(d, 1), :]
                for v in range(nvar):
                    row = met * flow_ref[k, v, pl.ds(d, 1), :]
                    vals = jnp.where(sub8 == v, row, vals)
                vhi = vals.astype(BF16).astype(F32)
                both = jnp.concatenate([vhi, vals - vhi], axis=0).astype(BF16)
                got = lax.dot_general(
                    jnp.concatenate([both, both], axis=1),
                    jnp.concatenate([hi, lo], axis=1),
                    (((1,), (1,)), ((), ())),
                    preferred_element_type=F32,
                )
                got = got[0:8] + got[8:16]
                got = got / got[nvar : nvar + 1, :]
                found.append((recv, jnp.where(e < n, got, 0.0)))
            for recv, got in found:
                first = pl.multiple_of(recv * 8, 8)
                acc[pl.ds(first, 8), :] += got

    for v in range(nvar):
        out_ref[v] = acc[pl.ds(v, radial, stride=8), :]


def local(offsets, flow, control_points, rbf_weights, peer_offset, donor_block, receptor_block):
    _, _, planes, radial, lines = offsets.shape
    nvar = flow.shape[1]
    nb = lax.axis_size("bulk")
    ng = lax.axis_size("grid")
    nd = nb * ng
    grid_here = lax.axis_index("grid")
    plane_ids = lax.axis_index("bulk") * planes + jnp.arange(planes, dtype=I32)
    base = lattice(grid_here[None], plane_ids, planes * nb, radial, lines) + offsets
    base = base.reshape(3, radial, lines)
    rows = control_points.shape[1] // 128
    points = jnp.concatenate([control_points, rbf_weights], axis=0).reshape(6 * rows, 128)
    slots = donor_block.shape[1]
    lrows = -(-slots // 128)
    spare = lrows * 128 - slots

    def lanes(x, fill):
        return jnp.pad(x.reshape(-1), (0, spare), constant_values=fill).reshape(lrows, 128)

    lists = jnp.concatenate(
        [lanes(peer_offset, -4 * ng), lanes(donor_block, 0), lanes(receptor_block, 0)], axis=0
    )
    dma = pltpu.SemaphoreType.DMA
    sds = jax.ShapeDtypeStruct
    many = nd + ng
    allp, alll, allf = pl.pallas_call(
        functools.partial(gather_kernel, nb, ng),
        out_shape=(
            sds((nd, 6 * rows, 128), F32),
            sds((ng, 3 * lrows, 128), I32),
            sds((ng, nvar, radial, lines), F32),
        ),
        in_specs=[VMEM_SPEC] * 3,
        out_specs=[VMEM_SPEC] * 3,
        scratch_shapes=[dma((many * 2,)), dma((nd,)), dma((many,)), dma((ng,)), dma((many,)), dma((ng,))],
        compiler_params=pltpu.CompilerParams(collective_id=0, has_side_effects=True),
        name="gather_points",
    )(points, lists, flow.reshape(nvar, radial, lines))
    nrow = ng * lrows
    moved, don, rec, num = pl.pallas_call(
        functools.partial(rbf_kernel, nd, rows, ng, lrows),
        out_shape=(
            sds((3, radial, lines), F32),
            sds((nrow, 128), I32),
            sds((nrow, 128), I32),
            sds((nrow, 128), I32),
        ),
        in_specs=[SMEM_SPEC] + [VMEM_SPEC] * 3,
        out_specs=[VMEM_SPEC] * 4,
        scratch_shapes=[
            pltpu.VMEM((6, nd * rows, 128), F32),
            pltpu.VMEM((6, 128, 128), F32),
            pltpu.VMEM((3, radial, 128), F32),
            pltpu.VMEM((6, radial, 8, 128), F32),
            pltpu.VMEM((6, radial * 8, 128), F32),
            pltpu.VMEM((radial * 8, 128), I32),
            pltpu.VMEM((radial, 128), I32),
            pltpu.SMEM((radial, 128), I32),
            pltpu.VMEM((3, radial, 128), F32),
            pltpu.VMEM((3, nrow, 128), I32),
            dma,
        ],
        cost_estimate=pl.CostEstimate(flops=200000000, bytes_accessed=500000, transcendentals=0),
        name="move_nodes",
    )(grid_here.reshape(1).astype(I32), base, allp, alll)
    metric, allm, allt = pl.pallas_call(
        functools.partial(metric_kernel, nb, ng),
        out_shape=(
            sds((radial, lines), F32),
            sds((ng, 3, radial, lines), F32),
            sds((ng, radial, lines), F32),
        ),
        in_specs=[VMEM_SPEC],
        out_specs=[VMEM_SPEC] * 3,
        scratch_shapes=[
            pltpu.VMEM((2, 3, radial, lines), F32),
            dma((2,)),
            dma((2,)),
            dma((2 * ng,)),
            dma((ng,)),
            dma((2 * ng,)),
            dma((ng,)),
        ],
        compiler_params=pltpu.CompilerParams(collective_id=1, has_side_effects=True),
        name="metric",
    )(moved)
    fringe = pl.pallas_call(
        blend_kernel,
        out_shape=sds((nvar, radial, lines), F32),
        in_specs=[SMEM_SPEC] * 3 + [VMEM_SPEC] * 4,
        out_specs=VMEM_SPEC,
        scratch_shapes=[
            pltpu.VMEM((radial, 3, 128, 128), F32),
            pltpu.VMEM((3, 128, 128), F32),
            pltpu.VMEM((radial * 8, 128), F32),
        ],
        name="blend",
    )(don, rec, num, moved, allm, allt, allf)
    return (
        moved.reshape(1, 3, planes, radial, lines),
        metric.reshape(1, planes, radial, lines),
        fringe.reshape(1, nvar, planes, radial, lines),
    )


def solution(mesh):
    in_specs = (
        P("grid", None, "bulk", None, None),
        P("grid", None, "bulk", None, None),
        P(None, ("bulk", "grid")),
        P(None, ("bulk", "grid")),
        P("grid", "bulk", None),
        P("grid", "bulk"),
        P("grid", "bulk"),
    )
    out_specs = (
        P("grid", None, "bulk", None, None),
        P("grid", "bulk", None, None),
        P("grid", None, "bulk", None, None),
    )
    return jax.shard_map(local, mesh=mesh, in_specs=in_specs, out_specs=out_specs, check_vma=False)
```

```python
import functools
import math

import jax
import jax.numpy as jnp
from jax import lax
from jax.experimental import pallas as pl
from jax.experimental.pallas import tpu as pltpu
from jax.sharding import PartitionSpec as P

MESH = pl.DeviceIdType.MESH
SUPPORT = 1.25
CULL = SUPPORT * SUPPORT * 1.0001
FAR = 1.0e9
UNROLL = 8
JOIN = 2
ENTRY_UNROLL = 4
F32 = jnp.float32
I32 = jnp.int32
BF16 = jnp.bfloat16
VMEM_SPEC = pl.BlockSpec(memory_space=pltpu.VMEM)
SMEM_SPEC = pl.BlockSpec(memory_space=pltpu.SMEM)


def lattice(grid_ids, plane_ids, planes_total, radial, lines):
    theta = 2.0 * math.pi * plane_ids.astype(jnp.float32) / planes_total
    radius = 1.0 + 0.25 * jnp.arange(radial, dtype=jnp.float32)
    height = 0.1 * jnp.arange(lines, dtype=jnp.float32)
    centre = 0.5 * grid_ids.astype(jnp.float32)
    xcoord = (
        centre[:, None, None, None]
        + radius[None, None, :, None] * jnp.cos(theta)[None, :, None, None]
        + 0.0 * height[None, None, None, :]
    )
    ycoord = (radius[None, :, None] * jnp.sin(theta)[:, None, None] + 0.0 * height[None, None, :])[
        None
    ] + 0.0 * centre[:, None, None, None]
    zcoord = jnp.zeros_like(xcoord) + height[None, None, None, :]
    return jnp.stack([xcoord, ycoord, zcoord], axis=1)


def take_lanes(x, idx):
    dims = lax.GatherDimensionNumbers(
        offset_dims=(),
        collapsed_slice_dims=(1,),
        start_index_map=(1,),
        operand_batching_dims=(0,),
        start_indices_batching_dims=(0,),
    )
    return lax.gather(
        x, idx[..., None], dims, slice_sizes=(1, 1), mode=lax.GatherScatterMode.PROMISE_IN_BOUNDS
    )


def iota(shape, axis):
    return lax.broadcasted_iota(I32, shape, axis)


def search(counts, target):
    pos = jnp.zeros(counts.shape, I32)
    step = counts.shape[1] // 2
    while step:
        seen = take_lanes(counts, pos + (step - 1))
        pos = jnp.where(seen <= target, pos + step, pos)
        step //= 2
    return pos


def halves(n):
    return (n // 2, 2) if n % 2 == 0 else (n, 1)


def line_and_pair(me, n):
    high, low = halves(n)
    place = lax.rem(me, low)
    line = [lax.rem(me // low + m, high) * low + place for m in range(1, high)]
    pair = [me + 1 - 2 * place] if low == 2 else []
    return line, pair


def gather_kernel(
    nb, ng, pts_ref, lst_ref, flow_ref, allp_ref, alll_ref, allf_ref, sp, rp, sl, rl, sf, rf
):
    b = lax.axis_index("bulk")
    g = lax.axis_index("grid")
    gline, gpair = line_and_pair(g, ng)
    bline, bpair = line_and_pair(b, nb)
    barrier = pltpu.get_barrier_semaphore()
    peers = [(b, t) for t in gline + gpair] + [(t, g) for t in bline + bpair]
    for peer in peers:
        pl.semaphore_signal(barrier, inc=1, device_id=peer, device_id_type=MESH)
    pl.semaphore_wait(barrier, len(peers))
    sent = {"p": [], "l": [], "f": []}

    def send(kind, slot, peer, own):
        source, full, ss, rs = {
            "p": (pts_ref, allp_ref, sp, rp),
            "l": (lst_ref, alll_ref, sl, rl),
            "f": (flow_ref, allf_ref, sf, rf),
        }[kind]
        copy = pltpu.make_async_remote_copy(
            src_ref=source if own else full.at[slot],
            dst_ref=full.at[slot],
            send_sem=ss.at[len(sent[kind])],
            recv_sem=rs.at[slot],
            device_id=peer,
            device_id_type=MESH,
        )
        copy.start()
        sent[kind].append(copy)

    def arrived(kind, slot):
        full, ss, rs = {
            "p": (allp_ref, sp, rp),
            "l": (alll_ref, sl, rl),
            "f": (allf_ref, sf, rf),
        }[kind]
        pltpu.make_async_remote_copy(
            src_ref=full.at[slot],
            dst_ref=full.at[slot],
            send_sem=ss.at[0],
            recv_sem=rs.at[slot],
            device_id=peers[0],
            device_id_type=MESH,
        ).wait_recv()

    def across(s, own):
        for t in bline + bpair:
            send("p", b * ng + s, (t, g), own)

    for t in gline + gpair:
        send("p", b * ng + g, (b, t), True)
    across(g, True)
    for kind in ("l", "f"):
        for t in gline + gpair:
            send(kind, g, (b, t), True)
    allp_ref[b * ng + g] = pts_ref[...]
    alll_ref[g] = lst_ref[...]
    for s in gline:
        arrived("p", b * ng + s)
        for t in gpair:
            send("p", b * ng + s, (b, t), False)
        across(s, False)
    for s in gline:
        for kind in ("l", "f"):
            arrived(kind, s)
            for t in gpair:
                send(kind, s, (b, t), False)
    low = halves(ng)[1]
    other = gpair + [t + gpair[0] - g for t in gline] if low == 2 else []
    for s in other:
        arrived("p", b * ng + s)
        across(s, False)
    for x in bline:
        for s in [g] + gline + other:
            arrived("p", x * ng + s)
            for t in bpair:
                send("p", x * ng + s, (t, g), False)
    for t in bpair:
        for x in [t] + [u + t - b for u in bline]:
            for s in [g] + gline + other:
                arrived("p", x * ng + s)
    for s in other:
        arrived("l", s)
        arrived("f", s)
    for kind in sent:
        for copy in sent[kind]:
            copy.wait_send()


def rbf_kernel(
    nd,
    rows,
    ng,
    lrows,
    here_ref,
    base_ref,
    pts_ref,
    lst_ref,
    moved_ref,
    don_ref,
    rec_ref,
    num_ref,
    pnt,
    fil,
    node,
    box,
    out,
    basec,
    cntv,
    cnts,
    shift,
    names,
    sem,
):
    radial = base_ref.shape[1]
    npat = radial // JOIN
    lane8 = iota((8, 128), 1)
    sub8 = iota((8, 128), 0)
    blocks_of_lanes = lane8 // 16
    within = lane8 - 16 * blocks_of_lanes
    upper = (iota((128, 128), 0) <= iota((128, 128), 1)).astype(F32).astype(BF16)

    def running(mask):
        return jnp.dot(
            mask.astype(F32).astype(BF16), upper, preferred_element_type=F32
        ).astype(I32)

    nrow = ng * lrows
    for k in range(ng):
        for c in range(3):
            names[c, k * lrows : (k + 1) * lrows, :] = lst_ref[k, c * lrows : (c + 1) * lrows, :]
    owner = iota((nrow, 128), 0) // lrows
    target = owner + 1 + names[0]
    target = jnp.where(target >= ng, target - ng, target)
    counts = running(target == here_ref[0])
    pos = search(counts, iota((nrow, 128), 1))
    don_ref[...] = owner * radial + take_lanes(names[1], pos)
    rec_ref[...] = take_lanes(names[2], pos)
    num_ref[...] = take_lanes(counts, jnp.full((nrow, 128), 127, I32))

    for d in range(nd):
        for c in range(6):
            pnt[c, d * rows : (d + 1) * rows, :] = pts_ref[d, c * rows : (c + 1) * rows, :]

    lows, highs = [], []
    for c in range(3):
        for jg in range(radial // 8):
            v = base_ref[c, 8 * jg : 8 * jg + 8, :]
            got = jnp.zeros((8, 128), F32)
            for j in range(8):
                row = jnp.broadcast_to(v[j : j + 1, :], (8, 128))
                got = jnp.where(blocks_of_lanes == j, take_lanes(row, 16 * sub8 + within), got)
            node[c, 8 * jg : 8 * jg + 8, :] = got
        full = node[c]
        lo = jnp.min(full, axis=1, keepdims=True)
        hi = jnp.max(full, axis=1, keepdims=True)
        for q in range(npat):
            mine = slice(q * JOIN, (q + 1) * JOIN)
            least = jnp.min(lo[mine], axis=0, keepdims=True)
            most = jnp.max(hi[mine], axis=0, keepdims=True)
            box[2 * c, q] = jnp.broadcast_to(least, (8, 128))
            box[2 * c + 1, q] = jnp.broadcast_to(most, (8, 128))
        lows.append(jnp.min(lo, axis=0, keepdims=True))
        highs.append(jnp.max(hi, axis=0, keepdims=True))

    dist = jnp.zeros((128, 128), F32)
    for c in range(3):
        p = pnt[c]
        e = jnp.maximum(jnp.maximum(lows[c] - p, p - highs[c]), 0.0)
        dist = dist + e * e
    counts = running(dist < CULL)
    lane = iota((128, 128), 1)
    pos = search(counts, lane)
    total = take_lanes(counts, jnp.full((128, 128), 127, I32))
    for c in range(6):
        v = take_lanes(pnt[c], pos)
        v = jnp.where(lane < total, v, FAR if c < 3 else 0.0)
        fil[c] = v.T
    groups = (jnp.max(total) + 7) // 8

    shift[...] = jnp.zeros(shift.shape, F32)
    cntv[...] = jnp.zeros(cntv.shape, I32)
    wide = npat * 8
    lane_w = iota((wide, 128), 1)

    def page_body(state):
        page, _ = state
        basec[...] = jnp.zeros(basec.shape, I32)
        out[...] = jnp.zeros(out.shape, F32)

        @pl.loop(0, groups)
        def _(gi):
            start = pl.multiple_of(gi * 8, 8)
            dist = jnp.zeros((npat, 8, 128), F32)
            for c in range(3):
                p = fil[c, pl.ds(start, 8), :][None]
                e = jnp.maximum(jnp.maximum(box[2 * c] - p, p - box[2 * c + 1]), 0.0)
                dist = dist + e * e
            before = basec[...]
            counts = before + running((dist < CULL).astype(F32).reshape(wide, 128))
            target = lane_w + 128 * page
            pos = search(counts, target)
            after = take_lanes(counts, jnp.full((wide, 128), 127, I32))
            keep = jnp.logical_and(target >= before, target < after)
            for c in range(6):
                src = jnp.broadcast_to(
                    fil[c, pl.ds(start, 8), :][None], (npat, 8, 128)
                ).reshape(wide, 128)
                out[c] = jnp.where(keep, take_lanes(src, pos), out[c])
            basec[...] = after

        most = jnp.max(basec[...].reshape(npat, 8, 128), axis=1)
        cntv[0:npat, :] = most
        copy = pltpu.make_async_copy(cntv, cnts, sem)
        copy.start()
        copy.wait()

        @pl.loop(0, npat)
        def _(p):
            n = jnp.minimum(cnts[p, 0] - 128 * page, 128)
            turns = (jnp.maximum(n, 0) + (UNROLL - 1)) // UNROLL
            at = [
                [
                    jnp.broadcast_to(node[c, pl.ds(p * JOIN + m, 1), :] * 0.8, (8, 128))
                    for c in range(3)
                ]
                for m in range(JOIN)
            ]
            first = pl.multiple_of(p * 8, 8)
            cols = [out[c, pl.ds(first, 8), :] for c in range(6)]
            cols = [v * 0.8 for v in cols[:3]] + cols[3:]

            def step(i, acc):
                acc = list(acc)
                for u in range(UNROLL):
                    idx = jnp.full((8, 128), i * UNROLL + u, I32)
                    px, py, pz, wx, wy, wz = [take_lanes(v, idx) for v in cols]
                    for m in range(JOIN):
                        dx = at[m][0] - px
                        dy = at[m][1] - py
                        dz = at[m][2] - pz
                        sq = jnp.maximum(dx * dx + dy * dy + dz * dz, 1e-30)
                        near = jnp.maximum(1.0 - sq * lax.rsqrt(sq), 0.0)
                        two = near * near
                        phi = two * two * (5.0 - 4.0 * near)
                        acc[3 * m] = acc[3 * m] + wx * phi
                        acc[3 * m + 1] = acc[3 * m + 1] + wy * phi
                        acc[3 * m + 2] = acc[3 * m + 2] + wz * phi
                return tuple(acc)

            zero = jnp.zeros((8, 128), F32)
            acc = lax.fori_loop(0, turns, step, (zero,) * (3 * JOIN))
            for m in range(JOIN):
                for c in range(3):
                    total_c = jnp.sum(acc[3 * m + c], axis=0, keepdims=True)
                    shift[c, pl.ds(p * JOIN + m, 1), :] += total_c

        return page + 1, jnp.max(most)

    lax.while_loop(
        lambda state: state[0] * 128 < state[1], page_body, (jnp.int32(0), jnp.int32(1))
    )

    for c in range(3):
        for jg in range(radial // 8):
            s = shift[c, 8 * jg : 8 * jg + 8, :]
            got = jnp.zeros((8, 128), F32)
            for kg in range(8):
                row = jnp.broadcast_to(s[kg : kg + 1, :], (8, 128))
                got = jnp.where(blocks_of_lanes == kg, take_lanes(row, 16 * sub8 + within), got)
            moved_ref[c, 8 * jg : 8 * jg + 8, :] = base_ref[c, 8 * jg : 8 * jg + 8, :] + got


def metric_kernel(nb, ng, mov_ref, met_ref, allm_ref, allt_ref, halo, sh, rh, sm, rm, st, rt):
    b = lax.axis_index("bulk")
    g = lax.axis_index("grid")
    after = lax.rem(b + 1, nb)
    before = lax.rem(b + nb - 1, nb)
    barrier = pltpu.get_barrier_semaphore()
    gline, gpair = line_and_pair(g, ng)
    peers = [(before, g), (after, g)] + [(b, t) for t in gline + gpair]
    for peer in peers:
        pl.semaphore_signal(barrier, inc=1, device_id=peer, device_id_type=MESH)
    pl.semaphore_wait(barrier, len(peers))
    halos = [
        pltpu.make_async_remote_copy(
            src_ref=mov_ref,
            dst_ref=halo.at[i],
            send_sem=sh.at[i],
            recv_sem=rh.at[i],
            device_id=(t, g),
            device_id_type=MESH,
        )
        for i, t in enumerate((after, before))
    ]
    for copy in halos:
        copy.start()

    sent = {"m": [], "t": []}

    def describe(kind, slot, peer, own, n):
        source, full, ss, rs = {
            "m": (mov_ref, allm_ref, sm, rm),
            "t": (met_ref, allt_ref, st, rt),
        }[kind]
        return pltpu.make_async_remote_copy(
            src_ref=source if own else full.at[slot],
            dst_ref=full.at[slot],
            send_sem=ss.at[n],
            recv_sem=rs.at[slot],
            device_id=peer,
            device_id_type=MESH,
        )

    def send(kind, slot, peer, own):
        copy = describe(kind, slot, peer, own, len(sent[kind]))
        copy.start()
        sent[kind].append(copy)

    for t in gline + gpair:
        send("m", g, (b, t), True)
    radial, lines = mov_ref.shape[1:]
    row = iota((radial, lines), 0)
    col = iota((radial, lines), 1)
    dj, dk = [], []
    for c in range(3):
        m = mov_ref[c]
        up, down = pltpu.roll(m, radial - 1, 0), pltpu.roll(m, 1, 0)
        dj.append(
            jnp.where(row == 0, up - m, jnp.where(row == radial - 1, m - down, (up - down) * 0.5))
        )
        up, down = pltpu.roll(m, lines - 1, 1), pltpu.roll(m, 1, 1)
        dk.append(
            jnp.where(col == 0, up - m, jnp.where(col == lines - 1, m - down, (up - down) * 0.5))
        )
    cross = [
        dj[1] * dk[2] - dj[2] * dk[1],
        dj[2] * dk[0] - dj[0] * dk[2],
        dj[0] * dk[1] - dj[1] * dk[0],
    ]
    for copy in halos:
        copy.wait_recv()
    di = [(halo[1, c] - halo[0, c]) * 0.5 for c in range(3)]
    met_ref[...] = di[0] * cross[0] + di[1] * cross[1] + di[2] * cross[2]
    for t in gline + gpair:
        send("t", g, (b, t), True)
    for kind in ("m", "t"):
        for s in gline:
            describe(kind, s, peers[0], False, 0).wait_recv()
            for t in gpair:
                send(kind, s, (b, t), False)
    other = gpair + [t + gpair[0] - g for t in gline] if gpair else []
    for kind in ("m", "t"):
        for s in other:
            describe(kind, s, peers[0], False, 0).wait_recv()
    for copy in halos + sent["m"] + sent["t"]:
        copy.wait_send()


def blend_kernel(
    don_ref, rec_ref, num_ref, mov_ref, allm_ref, allt_ref, flow_ref, out_ref, rep, tr, acc
):
    radial = mov_ref.shape[1]
    nvar = out_ref.shape[0]
    nrow = num_ref.shape[0]
    sub8 = iota((8, 128), 0)
    for c in range(3):
        tr[c] = jnp.zeros((128, 128), F32)
        tr[c, 0:radial, :] = mov_ref[c]
        tr[c] = tr[c].T

    @pl.loop(0, radial)
    def _(blk):
        idx = jnp.full((128, 128), blk, I32)
        for c in range(3):
            rep[blk, c] = take_lanes(tr[c], idx)

    acc[...] = jnp.zeros(acc.shape, F32)

    @pl.loop(0, nrow)
    def _(r):
        n = num_ref[r, 0]

        @pl.loop(0, (n + ENTRY_UNROLL - 1) // ENTRY_UNROLL)
        def _(i):
            found = []
            for u in range(ENTRY_UNROLL):
                e = i * ENTRY_UNROLL + u
                code = don_ref[r, e]
                recv = rec_ref[r, e]
                k = code // radial
                d = code - k * radial
                sq = None
                for c in range(3):
                    diff = rep[recv, c] - allm_ref[k, c, pl.ds(d, 1), :]
                    sq = diff * diff if sq is None else sq + diff * diff
                w = 1.0 / (0.25 + sq)
                hi = w.astype(BF16)
                lo = (w - hi.astype(F32)).astype(BF16)
                vals = jnp.where(sub8 == nvar, 1.0, jnp.zeros((8, 128), F32))
                met = allt_ref[k, pl.ds(d, 1), :]
                for v in range(nvar):
                    row = met * flow_ref[k, v, pl.ds(d, 1), :]
                    vals = jnp.where(sub8 == v, row, vals)
                vhi = vals.astype(BF16).astype(F32)
                both = jnp.concatenate([vhi, vals - vhi], axis=0).astype(BF16)
                got = lax.dot_general(
                    jnp.concatenate([both, both], axis=1),
                    jnp.concatenate([hi, lo], axis=1),
                    (((1,), (1,)), ((), ())),
                    preferred_element_type=F32,
                )
                got = got[0:8] + got[8:16]
                got = got / got[nvar : nvar + 1, :]
                found.append((recv, jnp.where(e < n, got, 0.0)))
            for recv, got in found:
                first = pl.multiple_of(recv * 8, 8)
                acc[pl.ds(first, 8), :] += got

    for v in range(nvar):
        out_ref[v] = acc[pl.ds(v, radial, stride=8), :]


def local(offsets, flow, control_points, rbf_weights, peer_offset, donor_block, receptor_block):
    _, _, planes, radial, lines = offsets.shape
    nvar = flow.shape[1]
    nb = lax.axis_size("bulk")
    ng = lax.axis_size("grid")
    nd = nb * ng
    grid_here = lax.axis_index("grid")
    plane_ids = lax.axis_index("bulk") * planes + jnp.arange(planes, dtype=I32)
    base = lattice(grid_here[None], plane_ids, planes * nb, radial, lines) + offsets
    base = base.reshape(3, radial, lines)
    rows = control_points.shape[1] // 128
    points = jnp.concatenate([control_points, rbf_weights], axis=0).reshape(6 * rows, 128)
    slots = donor_block.shape[1]
    lrows = -(-slots // 128)
    spare = lrows * 128 - slots

    def lanes(x, fill):
        return jnp.pad(x.reshape(-1), (0, spare), constant_values=fill).reshape(lrows, 128)

    lists = jnp.concatenate(
        [lanes(peer_offset, -4 * ng), lanes(donor_block, 0), lanes(receptor_block, 0)], axis=0
    )
    dma = pltpu.SemaphoreType.DMA
    sds = jax.ShapeDtypeStruct
    many = nd + ng
    allp, alll, allf = pl.pallas_call(
        functools.partial(gather_kernel, nb, ng),
        out_shape=(
            sds((nd, 6 * rows, 128), F32),
            sds((ng, 3 * lrows, 128), I32),
            sds((ng, nvar, radial, lines), F32),
        ),
        in_specs=[VMEM_SPEC] * 3,
        out_specs=[VMEM_SPEC] * 3,
        scratch_shapes=[dma((many * 2,)), dma((nd,)), dma((many,)), dma((ng,)), dma((many,)), dma((ng,))],
        compiler_params=pltpu.CompilerParams(collective_id=0, has_side_effects=True),
        name="gather_points",
    )(points, lists, flow.reshape(nvar, radial, lines))
    nrow = ng * lrows
    moved, don, rec, num = pl.pallas_call(
        functools.partial(rbf_kernel, nd, rows, ng, lrows),
        out_shape=(
            sds((3, radial, lines), F32),
            sds((nrow, 128), I32),
            sds((nrow, 128), I32),
            sds((nrow, 128), I32),
        ),
        in_specs=[SMEM_SPEC] + [VMEM_SPEC] * 3,
        out_specs=[VMEM_SPEC] * 4,
        scratch_shapes=[
            pltpu.VMEM((6, nd * rows, 128), F32),
            pltpu.VMEM((6, 128, 128), F32),
            pltpu.VMEM((3, radial, 128), F32),
            pltpu.VMEM((6, radial // JOIN, 8, 128), F32),
            pltpu.VMEM((6, radial // JOIN * 8, 128), F32),
            pltpu.VMEM((radial // JOIN * 8, 128), I32),
            pltpu.VMEM((radial, 128), I32),
            pltpu.SMEM((radial, 128), I32),
            pltpu.VMEM((3, radial, 128), F32),
            pltpu.VMEM((3, nrow, 128), I32),
            dma,
        ],
        cost_estimate=pl.CostEstimate(flops=200000000, bytes_accessed=500000, transcendentals=0),
        name="move_nodes",
    )(grid_here.reshape(1).astype(I32), base, allp, alll)
    metric, allm, allt = pl.pallas_call(
        functools.partial(metric_kernel, nb, ng),
        out_shape=(
            sds((radial, lines), F32),
            sds((ng, 3, radial, lines), F32),
            sds((ng, radial, lines), F32),
        ),
        in_specs=[VMEM_SPEC],
        out_specs=[VMEM_SPEC] * 3,
        scratch_shapes=[
            pltpu.VMEM((2, 3, radial, lines), F32),
            dma((2,)),
            dma((2,)),
            dma((2 * ng,)),
            dma((ng,)),
            dma((2 * ng,)),
            dma((ng,)),
        ],
        compiler_params=pltpu.CompilerParams(collective_id=1, has_side_effects=True),
        name="metric",
    )(moved)
    fringe = pl.pallas_call(
        blend_kernel,
        out_shape=sds((nvar, radial, lines), F32),
        in_specs=[SMEM_SPEC] * 3 + [VMEM_SPEC] * 4,
        out_specs=VMEM_SPEC,
        scratch_shapes=[
            pltpu.VMEM((radial, 3, 128, 128), F32),
            pltpu.VMEM((3, 128, 128), F32),
            pltpu.VMEM((radial * 8, 128), F32),
        ],
        name="blend",
    )(don, rec, num, moved, allm, allt, allf)
    return (
        moved.reshape(1, 3, planes, radial, lines),
        metric.reshape(1, planes, radial, lines),
        fringe.reshape(1, nvar, planes, radial, lines),
    )


def solution(mesh):
    in_specs = (
        P("grid", None, "bulk", None, None),
        P("grid", None, "bulk", None, None),
        P(None, ("bulk", "grid")),
        P(None, ("bulk", "grid")),
        P("grid", "bulk", None),
        P("grid", "bulk"),
        P("grid", "bulk"),
    )
    out_specs = (
        P("grid", None, "bulk", None, None),
        P("grid", "bulk", None, None),
        P("grid", None, "bulk", None, None),
    )
    return jax.shard_map(local, mesh=mesh, in_specs=in_specs, out_specs=out_specs, check_vma=False)
```
